256 devices in a mesh: lam: 128 (over z, y_hi, x, core), atom: 2 (over y_lo).
Axes of the slice: x: 4, y: 4 (y_hi: 2, y_lo: 2; y = y_hi * 2 + y_lo), z: 8, core: 2. Of those that a mesh axis runs over, the one named last changes fastest.
Arguments:
- coords: float32 [128, 3, 16384], P('lam', None, 'atom'), may hold values from 0 to 1
- velocities: float32 [128, 3, 16384], P('lam', None, 'atom'), may hold values from -6 to 6
- coupling: float32 [128, 2, 16384], P('lam', None, 'atom'), may hold values from 0.2 to 1
- charges: float32 [16384], replicated, may hold values from -1.5 to 1.5
- types: int32 [16384], replicated, may hold values from 0 to 15
- type_sigma: float32 [16], replicated, may hold values from 0.25 to 0.4
- type_eps: float32 [16], replicated, may hold values from 0.1 to 1
- near_tiles: int32 [128, 5], P('atom'), may hold values from 0 to 127
- accept: int32 [128], replicated, may hold values from 0 to 1, as said below
Outputs:
- energies: float32 [128, 3], P('lam')
- forces: float32 [128, 3, 16384], P('lam', None, 'atom')
- new_coords: float32 [128, 3, 16384], P('lam', None, 'atom')
- new_velocities: float32 [128, 3, 16384], P('lam', None, 'atom')
The draws below stay inside these ranges and needn't reach their ends.
Inputs may be any that keep to these rules, and one draw needn't show every extreme that they name: accept[r] = 1 exchanges replicas r and r + 1 (modulo 128); no two consecutive entries around the cycle are both 1.
All inputs are finite; a program needn't handle non-finite values.
Results may differ from the reference program's by a relative error of at most 0.0003.
Values sent between devices are 32-bit elements; how exact they have to be, the bound alone decides.
No kernel may reach another device: no remote copies, remote signals or barrier semaphores. Data moves between devices by JAX's collectives and lax.ppermute only.
A program may use at most 64 MiB of HBM per device.

```python
import math
from functools import partial
import jax
import jax.numpy as jnp
from jax import lax

TILE = 128
NEAR = 5
NTYPES = 16
REPLICAS = 128
ATOMS = 16384
TILES = 128


def draw_accept(key, part):
    coins = jax.random.randint(jax.random.fold_in(key, 11), (REPLICAS,), 0, 2)
    return (coins * (1 - jnp.roll(coins, 1))).astype(jnp.int32)


def touch_ends(drawn, own_key, smallest, high):
    extent = drawn.shape
    spot = [jax.random.randint(jax.random.fold_in(own_key, axis), (), 0, extent[axis]) for axis in range(len(extent))]
    drawn = drawn.at[tuple(spot)].set(smallest)
    longest = extent.index(max(extent))
    spot[longest] = (spot[longest] + 1) % extent[longest]
    return drawn.at[tuple(spot)].set(high)


def block_levels(key, dims, shards, low, high):
    level = 1.0
    for position, blocks in shards:
        steps = jax.random.uniform(jax.random.fold_in(jax.random.fold_in(key, 6), position), (blocks,), jnp.float32, low / len(shards), high / len(shards))
        level = level * jnp.repeat(jnp.exp(steps), dims[position] // blocks).reshape((-1,) + (1,) * (len(dims) - 1 - position))
    return level


def centred(stream_key, shape, scale, bound, split=(), held_as=jnp.bfloat16):
    factor_of = block_levels(stream_key, shape, split, -0.22, 0.18) if split else 1.0
    array = jax.random.normal(stream_key, shape, jnp.float32) * scale * factor_of
    return jnp.minimum(jnp.maximum(array, -bound), bound).astype(held_as)


def setup_inputs(seed: int = 0) -> dict:
    streams_of = jax.random.split(jax.random.key(seed), 10)
    coords = jnp.clip(1.0 * jax.random.uniform(streams_of[0], (REPLICAS, 3, ATOMS), jnp.float32) ** block_levels(streams_of[0], (REPLICAS, 3, ATOMS), ((0, 128), (2, 2)), -0.2, 0.2), 0.0, 1.0)
    velocities = centred(streams_of[1], (REPLICAS, 3, ATOMS), 1.0, 6.0, ((0, 128), (2, 2)), jnp.float32)
    coupling = jnp.clip(jnp.exp(math.log(1.0) - 1.609438 * jax.random.uniform(streams_of[2], (REPLICAS, 2, ATOMS), jnp.float32) ** block_levels(streams_of[2], (REPLICAS, 2, ATOMS), ((0, 128), (2, 2)), -0.2, 0.2)), 0.2, 1.0)
    charges = centred(streams_of[3], (ATOMS,), 0.3, 1.5, (), jnp.float32)
    types = touch_ends(jax.random.randint(streams_of[4], (ATOMS,), 0, NTYPES), jax.random.fold_in(streams_of[4], 1), 0, NTYPES - 1).astype(jnp.int32)
    type_sigma = jnp.clip(jnp.exp(jax.random.uniform(streams_of[5], (NTYPES,), jnp.float32, math.log(0.25), math.log(0.4))), 0.25, 0.4)
    type_eps = jnp.clip(jnp.exp(jax.random.uniform(streams_of[6], (NTYPES,), jnp.float32, math.log(0.1), math.log(1.0))), 0.1, 1.0)
    near_tiles = touch_ends(jax.random.randint(streams_of[7], (TILES, NEAR), 0, TILES), jax.random.fold_in(streams_of[7], 1), 0, TILES - 1).astype(jnp.int32)
    accept = draw_accept(jax.random.fold_in(streams_of[9], 71), 0)
    return dict(coords=coords, velocities=velocities, coupling=coupling, charges=charges, types=types, type_sigma=type_sigma, type_eps=type_eps, near_tiles=near_tiles, accept=accept)


DELTA_SOFT = 0.05

def atom_params(charges, types, type_sigma, type_eps, coupling_whole):
    levels = lax.broadcasted_iota(jnp.int32, (type_sigma.shape[0], types.shape[0]), 0)
    onehot = (levels == types[None, :]).astype(jnp.float32)
    table = jnp.stack([type_sigma, jnp.sqrt(type_eps)])
    looked = jnp.dot(table, onehot, precision=lax.Precision.HIGHEST)
    return jnp.stack([charges * coupling_whole[0], looked[1] * coupling_whole[1], looked[0]])

def pair_block(inputs, with_force):
    rows_pos, cols_pos, rows_par, cols_par, rows_idx, cols_idx = inputs
    delta = rows_pos[:, :, None, :, None] - cols_pos[:, :, :, None, :]
    squared = lax.optimization_barrier(jnp.sum(delta * delta, axis=0))
    charge_pair = rows_par[0][:, None, :, None] * cols_par[0][:, :, None, :]
    depth_pair = rows_par[1][:, None, :, None] * cols_par[1][:, :, None, :]
    sigma_pair = 0.5 * (rows_par[2][:, None, :, None] + cols_par[2][:, :, None, :])
    sigma_area = sigma_pair * sigma_pair
    pair_keep = (rows_idx[:, None, :, None] != cols_idx[:, :, None, :]).astype(jnp.float32)
    inverse = lax.rsqrt(squared + DELTA_SOFT)
    ratio = sigma_area / (squared + sigma_area)
    cubed = ratio * ratio * ratio
    energy_pair = charge_pair * inverse + 4.0 * depth_pair * (cubed * cubed - cubed)
    total = jnp.sum(energy_pair * pair_keep)
    if not with_force:
        return (total, jnp.zeros_like(rows_pos))
    slope = -0.5 * charge_pair * inverse * inverse * inverse - 4.0 * depth_pair * (6.0 * cubed * ratio * ratio - 3.0 * ratio * ratio) * ratio * ratio / sigma_area
    weight = -2.0 * slope * pair_keep
    force = lax.optimization_barrier(jnp.sum(weight[None] * delta, axis=(2, 4)))
    return (total, force)

def evaluate(own_rows, whole, params, first_row, tile_list, with_force):
    count = own_rows.shape[1]
    row_tiles = count // TILE
    group = math.gcd(row_tiles, 4)
    blocks = row_tiles // group
    listed = tile_list.shape[1]
    rows_pos = own_rows.reshape(3, blocks, group, TILE).transpose(1, 0, 2, 3)
    own_par = lax.dynamic_slice_in_dim(params, first_row, count, 1)
    rows_par = own_par.reshape(3, blocks, group, TILE).transpose(1, 0, 2, 3)
    cols_pos = whole.reshape(3, -1, TILE)[:, tile_list].reshape(3, blocks, group, listed, TILE).transpose(1, 0, 2, 3, 4)
    cols_par = params.reshape(3, -1, TILE)[:, tile_list].reshape(3, blocks, group, listed, TILE).transpose(1, 0, 2, 3, 4)
    rows_idx = (first_row + jnp.arange(count, dtype=jnp.int32)).reshape(blocks, group, TILE)
    cols_idx = (tile_list[:, :, None] * TILE + jnp.arange(TILE, dtype=jnp.int32)[None, None, :]).reshape(blocks, group, listed, TILE)
    totals, forces = lax.map(partial(pair_block, with_force=with_force), (rows_pos, cols_pos, rows_par, cols_par, rows_idx, cols_idx))
    return (jnp.sum(totals), forces.transpose(1, 0, 2, 3).reshape(3, count))

def reference(coords, velocities, coupling, charges, types, type_sigma, type_eps, near_tiles, accept):
    count = coords.shape[0]

    def replica_terms(index):
        params = atom_params(charges, types, type_sigma, type_eps, coupling[index])
        own_coords = coords[index]
        lower_coords = coords[(index + count - 1) % count]
        upper_coords = coords[(index + 1) % count]
        energy_own, force = evaluate(own_coords, own_coords, params, 0, near_tiles, True)
        energy_low, unused = evaluate(lower_coords, lower_coords, params, 0, near_tiles, False)
        energy_up, unused = evaluate(upper_coords, upper_coords, params, 0, near_tiles, False)
        return (jnp.stack([energy_own, energy_low, energy_up]), force)
    totals_all, forces = lax.map(replica_terms, jnp.arange(count, dtype=jnp.int32))
    scale = 0.5 / ATOMS
    energies = jnp.stack([totals_all[:, 0], jnp.roll(totals_all[:, 2], 1), jnp.roll(totals_all[:, 1], -1)], axis=1) * scale
    upper_flag = (accept == 1)[:, None, None]
    lower_flag = (jnp.roll(accept, 1) == 1)[:, None, None]
    new_coords = jnp.where(upper_flag, jnp.roll(coords, -1, axis=0), jnp.where(lower_flag, jnp.roll(coords, 1, axis=0), coords))
    new_velocities = jnp.where(upper_flag, jnp.roll(velocities, -1, axis=0), jnp.where(lower_flag, jnp.roll(velocities, 1, axis=0), velocities))
    return (energies, forces, new_coords, new_velocities)
```

```python
from functools import partial

import jax
import jax.numpy as jnp
from jax import lax
from jax.experimental import pallas as pl
from jax.experimental.pallas import tpu as pltpu
from jax.sharding import PartitionSpec as P

TILE = 128
DELTA_SOFT = 0.05


def passed_along(x, axis, by):
    peers = lax.axis_size(axis)
    return lax.ppermute(x, axis, [(i, (i + by) % peers) for i in range(peers)])


def passed_across(x, by):
    cycle = lax.axis_size("lam")
    halves = lax.axis_size("atom")
    pairs = [
        (r * halves + a, ((r + by) % cycle) * halves + (a + 1) % halves)
        for r in range(cycle)
        for a in range(halves)
    ]
    return lax.ppermute(x, ("lam", "atom"), pairs)


def split3(z):
    one = z.astype(jnp.bfloat16)
    rest = z - one.astype(jnp.float32)
    two = rest.astype(jnp.bfloat16)
    rest = rest - two.astype(jnp.float32)
    return one, two, rest.astype(jnp.bfloat16)


def split2(z):
    one = z.astype(jnp.bfloat16)
    two = (z - one.astype(jnp.float32)).astype(jnp.bfloat16)
    return one, two


def tile_kernel(
    near_ref,
    pos_ref, cpl_ref, low_ref, up_ref,
    pos2_ref, cpl2_ref, low2_ref, up2_ref,
    look_ref,
    energy_ref, force_ref,
    feat_ref, side_ref, vec_ref, zc_ref, ze_ref,
    *, half, listed,
):
    first = near_ref[half * listed]

    def prepare(t, pos_from, cpl_from, low_from, up_from, own):
        lanes = pl.ds(pl.multiple_of(t * TILE, TILE), TILE)
        there = t + (first if own else half - first)
        dest = t if own else t + half
        looked = look_ref[:, pl.ds(pl.multiple_of(there * TILE, TILE), TILE)]
        pos = pos_from[:, lanes]
        charge0, depth0, h = looked[0:1], looked[1:2], looked[2:3]
        cpl, low, up = cpl_from[:, lanes], low_from[:, lanes], up_from[:, lanes]
        sq = pos * pos
        n = sq[0:1] + sq[1:2] + sq[2:3]
        h2 = h * h
        one = jnp.ones_like(n)
        zero = jnp.zeros_like(n)
        feats = jnp.concatenate([pos, n, h, h2, one, zero], axis=0)
        p1, p2, p3 = split3(feats)
        feat_ref[dest] = jnp.concatenate([p1, p1, p2, p2, p1, p3], axis=0)
        c0 = charge0 * cpl[0:1]
        e0 = depth0 * cpl[1:2]
        zc = jnp.concatenate(
            [c0, charge0 * low[0:1], charge0 * up[0:1], c0 * pos, zero, zero], axis=0
        )
        ze = jnp.concatenate(
            [e0, depth0 * low[1:2], depth0 * up[1:2], e0 * pos, zero, zero], axis=0
        )
        c1, c2 = split2(zc)
        e1, e2 = split2(ze)
        vec_ref[dest] = jnp.concatenate([c1, c2, e1, e2], axis=0)
        if own:
            zc_ref[dest] = zc
            ze_ref[dest] = ze
            m = -2.0 * pos
            hh = 2.0 * h
            sides = jnp.concatenate(
                [
                    jnp.concatenate([m, one, zero, zero, n + DELTA_SOFT, zero], axis=0),
                    jnp.concatenate([m, one, hh, one, n + h2, zero], axis=0),
                    jnp.concatenate([zero, zero, zero, zero, hh, one, h2, zero], axis=0),
                ],
                axis=1,
            )
            q1, q2, q3 = split3(sides)
            side_ref[dest] = jnp.concatenate([q1, q2, q1, q2, q3, q1], axis=0)

    def prep_own(t, _):
        prepare(t, pos_ref, cpl_ref, low_ref, up_ref, True)
        return 0

    def prep_other(t, _):
        prepare(t, pos2_ref, cpl2_ref, low2_ref, up2_ref, False)
        return 0

    lax.fori_loop(0, half, prep_own, 0)
    lax.fori_loop(0, half, prep_other, 0)

    def pair_sums(i, total):
        side = side_ref[i]
        acc = [jnp.zeros((16, TILE), jnp.float32) for _ in range(4)]
        own_times = jnp.int32(0)
        for k in range(listed):
            c = near_ref[i * listed + k]
            own_times = own_times + jnp.where(c == i, 1, 0)
            feat = feat_ref[c]
            vec = vec_ref[c]
            stg = lax.dot_general(
                feat, side, (((0,), (0,)), ((), ())), preferred_element_type=jnp.float32
            )
            s, t, g = stg[:, :TILE], stg[:, TILE : 2 * TILE], stg[:, 2 * TILE :]
            inv = lax.rsqrt(s)
            rt = 1.0 / t
            x = g * rt
            x3 = x * x * x
            p = x3 * (x3 - 0.5)
            b = x3 * (x3 - 1.0)
            f = p * rt
            inv3 = inv * inv * inv
            cc = jnp.concatenate([vec[:16], vec[:16]], axis=1)
            ee = jnp.concatenate([vec[16:], vec[16:]], axis=1)
            for n, (lhs, mat) in enumerate(((cc, inv), (ee, b), (cc, inv3), (ee, f))):
                hi, lo = split2(mat)
                acc[n] = acc[n] + jnp.dot(
                    lhs, jnp.concatenate([hi, lo], axis=0), preferred_element_type=jnp.float32
                )
        sum_a, sum_b, sum_i, sum_f = [a[:8] + a[8:] for a in acc]
        zc = zc_ref[i]
        ze = ze_ref[i]
        own = own_times.astype(jnp.float32) * (DELTA_SOFT**-0.5)
        total = total + zc * (sum_a - own * zc) + 4.0 * (ze * sum_b)
        lanes = pl.ds(pl.multiple_of(i * TILE, TILE), TILE)
        pos = pos_ref[:, lanes]
        force = zc[0:1] * (pos * sum_i[0:1] - sum_i[3:6]) + 48.0 * ze[0:1] * (
            pos * sum_f[0:1] - sum_f[3:6]
        )
        force_ref[:, lanes] = force
        return total

    total = lax.fori_loop(0, half, pair_sums, jnp.zeros((8, TILE), jnp.float32))
    energy_ref[...] = jnp.broadcast_to(jnp.sum(total, axis=1, keepdims=True), (8, TILE))


def lookup(charges, types, type_sigma, type_eps):
    levels = lax.broadcasted_iota(jnp.int32, (type_sigma.shape[0], types.shape[0]), 0)
    onehot = (levels == types[None, :]).astype(jnp.float32)
    table = jnp.stack([jnp.sqrt(type_eps), 0.5 * type_sigma])
    looked = jnp.dot(table, onehot, precision=lax.Precision.HIGHEST)
    return jnp.concatenate([charges[None], looked])


def call_kernel(args, half, listed):
    width = half * TILE
    tiles = 2 * half
    vmem = pl.BlockSpec(memory_space=pltpu.VMEM)
    return pl.pallas_call(
        partial(tile_kernel, half=half, listed=listed),
        out_shape=(
            jax.ShapeDtypeStruct((8, TILE), jnp.float32),
            jax.ShapeDtypeStruct((3, width), jnp.float32),
        ),
        in_specs=[pl.BlockSpec(memory_space=pltpu.SMEM)] + [vmem] * 9,
        out_specs=(vmem, vmem),
        scratch_shapes=[
            pltpu.VMEM((tiles, 48, TILE), jnp.bfloat16),
            pltpu.VMEM((half, 48, 3 * TILE), jnp.bfloat16),
            pltpu.VMEM((tiles, 32, TILE), jnp.bfloat16),
            pltpu.VMEM((half, 8, TILE), jnp.float32),
            pltpu.VMEM((half, 8, TILE), jnp.float32),
        ],
        compiler_params=pltpu.CompilerParams(vmem_limit_bytes=40 * 2**20),
        name="tiles",
    )(*args)


def per_device(
    coords, velocities, coupling, charges, types, type_sigma, type_eps, near_tiles, accept
):
    pos = coords[0]
    moving = velocities[0]
    cpl = coupling[0]
    width = pos.shape[1]
    half = width // TILE
    atoms = charges.shape[0]
    listed = near_tiles.shape[1]
    pos2 = passed_along(pos, "atom", 1)
    cpl2 = passed_along(cpl, "atom", 1)
    low = passed_along(cpl, "lam", 1)
    up = passed_along(cpl, "lam", -1)
    low2 = passed_across(cpl, 1)
    up2 = passed_across(cpl, -1)
    lower_coords, lower_moving = passed_along((pos, moving), "lam", 1)
    upper_coords, upper_moving = passed_along((pos, moving), "lam", -1)

    look = lookup(charges, types, type_sigma, type_eps)
    first = lax.axis_index("atom") * half
    tiles = 2 * half
    local = jnp.mod(near_tiles.reshape(-1) - first + tiles, tiles)
    near = jnp.concatenate([local, first[None]]).astype(jnp.int32)

    energy, force = call_kernel(
        (near, pos, cpl, low, up, pos2, cpl2, low2, up2, look), half, listed
    )

    part = energy[:3, 0] * (0.5 / atoms)
    energies = (part + passed_along(part, "atom", 1))[None]
    replica = lax.axis_index("lam")
    cycle_size = lax.axis_size("lam")
    upper_flag = accept[replica] == 1
    lower_flag = accept[(replica + cycle_size - 1) % cycle_size] == 1
    new_coords = jnp.where(upper_flag, upper_coords, jnp.where(lower_flag, lower_coords, pos))
    new_velocities = jnp.where(
        upper_flag, upper_moving, jnp.where(lower_flag, lower_moving, moving)
    )
    return (energies, force[None], new_coords[None], new_velocities[None])


def solution(mesh):
    in_specs = (
        P("lam", None, "atom"),
        P("lam", None, "atom"),
        P("lam", None, "atom"),
        P(),
        P(),
        P(),
        P(),
        P("atom", None),
        P(),
    )
    out_specs = (
        P("lam", None),
        P("lam", None, "atom"),
        P("lam", None, "atom"),
        P("lam", None, "atom"),
    )
    return jax.shard_map(
        per_device, mesh=mesh, in_specs=in_specs, out_specs=out_specs, check_vma=False
    )
```

```python
from functools import partial

import jax
import jax.numpy as jnp
from jax import lax
from jax.experimental import pallas as pl
from jax.experimental.pallas import tpu as pltpu
from jax.sharding import PartitionSpec as P

TILE = 128
DELTA_SOFT = 0.05
CHUNK = 32
RING = 5
AHEAD = 3
LATE = 2
ROWS = 4


def swapped(x, axis, first):
    peers = lax.axis_size(axis)
    pairs = []
    for i in range(first, peers + first, 2):
        low, high = i % peers, (i + 1) % peers
        pairs += [(low, high), (high, low)]
    return lax.ppermute(x, axis, pairs)


def split3(z):
    one = z.astype(jnp.bfloat16)
    rest = z - one.astype(jnp.float32)
    two = rest.astype(jnp.bfloat16)
    rest = rest - two.astype(jnp.float32)
    return one, two, rest.astype(jnp.bfloat16)


def split2(z):
    one = z.astype(jnp.bfloat16)
    two = (z - one.astype(jnp.float32)).astype(jnp.bfloat16)
    return one, two


def tile_kernel(
    near_ref,
    five_ref, moving_ref, other_ref, pair1_ref, pair2_ref, look_ref,
    energy_ref, force_ref, coords_out, moving_out,
    feat_ref, side_ref, vec_ref, zc_ref, ze_ref, pos_ref, new_ref, sem, *work_refs,
    half, listed,
):
    first = near_ref[half * listed]
    take1 = near_ref[half * listed + 1] == 1
    take2 = near_ref[half * listed + 2] == 1
    dist_refs, mat_refs = work_refs[:RING], work_refs[RING:]

    def prepare(t, from_ref, at, own):
        def rows(ref, *js):
            return [ref[j, pl.ds(t, 1), :] for j in js]

        there = t + (first if own else half - first)
        dest = t if own else t + half
        charge0, depth0, h = [look_ref[j, pl.ds(there, 1), :] for j in range(3)]
        x, y, z, cpl0, cpl1 = rows(from_ref, *range(5))
        low0, low1 = rows(pair1_ref, at, at + 1)
        up0, up1 = rows(pair2_ref, at, at + 1)
        n = x * x + y * y + z * z
        h2 = h * h
        one = jnp.ones_like(n)
        zero = jnp.zeros_like(n)
        feats = jnp.concatenate([x, y, z, n, h, h2, one, zero], axis=0)
        p1, p2, p3 = split3(feats)
        feat_ref[dest] = jnp.concatenate([p1, p1, p2, p2, p1, p3], axis=0)
        c0 = charge0 * cpl0
        e0 = depth0 * cpl1
        pos = feats[0:3]
        zc = jnp.concatenate([c0, charge0 * low0, charge0 * up0, c0 * pos, zero, zero], axis=0)
        ze = jnp.concatenate([e0, depth0 * low1, depth0 * up1, e0 * pos, zero, zero], axis=0)
        c1, c2 = split2(zc)
        e1, e2 = split2(ze)
        vec_ref[dest] = jnp.concatenate([c1, c2, e1, e2], axis=0)
        if own:
            zc_ref[dest] = zc
            ze_ref[dest] = ze
            pos_ref[dest] = feats
            m = -2.0 * pos
            hh = 2.0 * h
            sides = jnp.concatenate(
                [
                    jnp.concatenate([m, one, zero, zero, n + DELTA_SOFT, zero], axis=0),
                    jnp.concatenate([m, one, hh, one, n + h2, zero], axis=0),
                    jnp.concatenate([zero, zero, zero, zero, hh, one, h2, zero], axis=0),
                ],
                axis=1,
            )
            q1, q2, q3 = split3(sides)
            side_ref[dest] = jnp.concatenate([q1, q2, q1, q2, q3, q1], axis=0)
            lanes = pl.ds(pl.multiple_of(t * TILE, TILE), TILE)
            own_rows = [x, y, z] + rows(moving_ref, *range(3))
            for n, (mine, one_row, two_row) in enumerate(
                zip(own_rows, rows(pair1_ref, *range(4, 10)), rows(pair2_ref, *range(4, 10)))
            ):
                new_ref[n // 3, pl.ds(n % 3, 1), lanes] = jnp.where(
                    take1, one_row, jnp.where(take2, two_row, mine)
                )

    def prep_own(t, _):
        prepare(t, five_ref, 0, True)
        return 0

    def prep_other(t, _):
        prepare(t, other_ref, 2, False)
        return 0

    lax.fori_loop(0, half, prep_own, 0)
    copies = [
        pltpu.make_async_copy(new_ref.at[n], out, sem.at[n])
        for n, out in enumerate((coords_out, moving_out))
    ]
    for copy in copies:
        copy.start()
    lax.fori_loop(0, half, prep_other, 0)

    def distances(i, k):
        c = near_ref[i * listed + k]
        dist_refs[k % RING][...] = lax.dot_general(
            feat_ref[c], side_ref[i], (((0,), (0,)), ((), ())),
            preferred_element_type=jnp.float32,
        )

    def functions(k):
        dist_ref, mat_ref = dist_refs[k % RING], mat_refs[k % RING]
        for r in range(0, TILE, CHUNK):
            rows = slice(r, r + CHUNK)
            low_rows = slice(TILE + r, TILE + r + CHUNK)
            s = dist_ref[rows, :TILE]
            t = dist_ref[rows, TILE : 2 * TILE]
            g = dist_ref[rows, 2 * TILE :]
            inv = lax.rsqrt(s)
            rt = 1.0 / t
            x = g * rt
            x3 = x * x * x
            f = x3 * (x3 - 0.5) * rt
            b = x3 * (x3 - 1.0)
            for n, mat in enumerate((inv, b, inv * inv * inv, f)):
                hi, lo = split2(mat)
                mat_ref[n, rows] = hi
                mat_ref[n, low_rows] = lo

    def gather(i, k, acc):
        vec = vec_ref[near_ref[i * listed + k]]
        cc = jnp.concatenate([vec[:16], vec[:16]], axis=1)
        ee = jnp.concatenate([vec[16:], vec[16:]], axis=1)
        mat_ref = mat_refs[k % RING]
        return [
            a + jnp.dot(lhs, mat_ref[n], preferred_element_type=jnp.float32)
            for n, (a, lhs) in enumerate(zip(acc, (cc, ee, cc, ee)))
        ]

    def finish(i, acc, total):
        sum_a, sum_b, sum_i, sum_f = [a[:8] + a[8:] for a in acc]
        own_times = jnp.int32(0)
        for k in range(listed):
            own_times = own_times + jnp.where(near_ref[i * listed + k] == i, 1, 0)
        zc = zc_ref[i]
        ze = ze_ref[i]
        own = own_times.astype(jnp.float32) * (DELTA_SOFT**-0.5)
        lanes = pl.ds(pl.multiple_of(i * TILE, TILE), TILE)
        pos = pos_ref[i, 0:3]
        force_ref[:, lanes] = zc[0:1] * (pos * sum_i[0:1] - sum_i[3:6]) + 48.0 * ze[0:1] * (
            pos * sum_f[0:1] - sum_f[3:6]
        )
        return total + zc * (sum_a - own * zc) + 4.0 * (ze * sum_b)

    def nothing():
        return [jnp.zeros((16, TILE), jnp.float32) for _ in range(4)]

    def row(i, acc, total):
        behind = jnp.maximum(i - 1, 0)
        following = jnp.minimum(i + 1, half - 1)
        for k in range(listed - LATE, listed):
            acc = gather(behind, k, acc)
        done = finish(behind, acc, total)
        total = jnp.where(i > 0, done, total)
        acc = nothing()
        for k in range(listed):
            if k + AHEAD < listed:
                distances(i, k + AHEAD)
            functions(k)
            if k + AHEAD >= listed:
                distances(following, k + AHEAD - listed)
            if k < listed - LATE:
                acc = gather(i, k, acc)
        return acc, total

    def next_rows(step, carry):
        for j in range(ROWS):
            carry = row(step * ROWS + j, *carry)
        return carry

    for k in range(AHEAD):
        distances(0, k)
    for k in range(listed - LATE, listed):
        mat_refs[k][...] = jnp.zeros_like(mat_refs[k])
    acc, total = lax.fori_loop(
        0, half // ROWS, next_rows, (nothing(), jnp.zeros((8, TILE), jnp.float32))
    )
    for k in range(listed - LATE, listed):
        acc = gather(half - 1, k, acc)
    total = finish(half - 1, acc, total)
    energy_ref[...] = jnp.broadcast_to(jnp.sum(total, axis=1, keepdims=True), (8, TILE))
    for copy in copies:
        copy.wait()


def lookup(charges, types, type_sigma, type_eps):
    levels = lax.broadcasted_iota(jnp.int32, (type_sigma.shape[0], types.shape[0]), 0)
    onehot = (levels == types[None, :]).astype(jnp.float32)
    table = jnp.stack([jnp.sqrt(type_eps), 0.5 * type_sigma])
    looked = jnp.dot(table, onehot, precision=lax.Precision.HIGHEST)
    return jnp.concatenate([charges[None], looked])


def call_kernel(args, half, listed):
    width = half * TILE
    tiles = 2 * half
    vmem = pl.BlockSpec(memory_space=pltpu.VMEM)
    hbm = pl.BlockSpec(memory_space=pltpu.HBM)
    return pl.pallas_call(
        partial(tile_kernel, half=half, listed=listed),
        out_shape=(
            jax.ShapeDtypeStruct((8, TILE), jnp.float32),
            jax.ShapeDtypeStruct((3, width), jnp.float32),
            jax.ShapeDtypeStruct((3, width), jnp.float32),
            jax.ShapeDtypeStruct((3, width), jnp.float32),
        ),
        in_specs=[pl.BlockSpec(memory_space=pltpu.SMEM)] + [vmem] * 6,
        out_specs=(vmem, vmem, hbm, hbm),
        scratch_shapes=[
            pltpu.VMEM((tiles, 48, TILE), jnp.bfloat16),
            pltpu.VMEM((half, 48, 3 * TILE), jnp.bfloat16),
            pltpu.VMEM((tiles, 32, TILE), jnp.bfloat16),
            pltpu.VMEM((half, 8, TILE), jnp.float32),
            pltpu.VMEM((half, 8, TILE), jnp.float32),
            pltpu.VMEM((half, 8, TILE), jnp.float32),
            pltpu.VMEM((2, 3, width), jnp.float32),
            pltpu.SemaphoreType.DMA((2,)),
        ]
        + [pltpu.VMEM((TILE, 3 * TILE), jnp.float32)] * RING
        + [pltpu.VMEM((4, 2 * TILE, TILE), jnp.bfloat16)] * RING,
        compiler_params=pltpu.CompilerParams(vmem_limit_bytes=40 * 2**20),
        name="tiles",
    )(*args)


def per_device(
    coords, velocities, coupling, charges, types, type_sigma, type_eps, near_tiles, accept
):
    width = coords.shape[2]
    half = width // TILE
    atoms = charges.shape[0]
    listed = near_tiles.shape[1]
    pos = coords.reshape(3, half, TILE)
    moving = velocities.reshape(3, half, TILE)
    cpl = coupling.reshape(2, half, TILE)
    five = jnp.concatenate([pos, cpl])
    other = swapped(five, "atom", 0)
    ten = jnp.concatenate([cpl, other[3:], pos, moving])
    pair1 = swapped(ten, "lam", 0)
    pair2 = swapped(ten, "lam", 1)

    look = lookup(charges, types, type_sigma, type_eps).reshape(3, 2 * half, TILE)
    first = lax.axis_index("atom") * half
    tiles = 2 * half
    local = jnp.mod(near_tiles.reshape(-1) - first + tiles, tiles)
    replica = lax.axis_index("lam")
    cycle = lax.axis_size("lam")
    odd = replica % 2
    flag1 = accept[replica - odd]
    flag2 = accept[jnp.mod(replica - 1 + odd + cycle, cycle)]
    near = jnp.concatenate([local, jnp.stack([first, flag1, flag2])]).astype(jnp.int32)

    energy, force, new_coords, new_velocities = call_kernel(
        (near, five, moving, other, pair1, pair2, look), half, listed
    )
    part = energy[:3, 0] * (0.5 / atoms)
    whole = part + swapped(part, "atom", 0)
    one, two = whole[1], whole[2]
    energies = jnp.stack([whole[0], jnp.where(odd == 1, one, two), jnp.where(odd == 1, two, one)])
    return (energies[None], force[None], new_coords[None], new_velocities[None])


def solution(mesh):
    in_specs = (
        P("lam", None, "atom"),
        P("lam", None, "atom"),
        P("lam", None, "atom"),
        P(),
        P(),
        P(),
        P(),
        P("atom", None),
        P(),
    )
    out_specs = (
        P("lam", None),
        P("lam", None, "atom"),
        P("lam", None, "atom"),
        P("lam", None, "atom"),
    )
    return jax.shard_map(
        per_device, mesh=mesh, in_specs=in_specs, out_specs=out_specs, check_vma=False
    )
```

```python
from functools import partial

import jax
import jax.numpy as jnp
from jax import lax
from jax.experimental import pallas as pl
from jax.experimental.pallas import tpu as pltpu
from jax.sharding import PartitionSpec as P

TILE = 128
DELTA_SOFT = 0.05
CHUNK = 32
RING = 5
AHEAD = 3
LATE = 2
ROWS = 16
PREP = 8


def swapped(x, axis, first):
    peers = lax.axis_size(axis)
    pairs = []
    for i in range(first, peers + first, 2):
        low, high = i % peers, (i + 1) % peers
        pairs += [(low, high), (high, low)]
    return lax.ppermute(x, axis, pairs)


def split3(z):
    one = z.astype(jnp.bfloat16)
    rest = z - one.astype(jnp.float32)
    two = rest.astype(jnp.bfloat16)
    rest = rest - two.astype(jnp.float32)
    return one, two, rest.astype(jnp.bfloat16)


def split2(z):
    one = z.astype(jnp.bfloat16)
    two = (z - one.astype(jnp.float32)).astype(jnp.bfloat16)
    return one, two


def tile_kernel(
    near_ref,
    five_ref, moving_ref, other_ref, pair1_ref, pair2_ref, look_ref,
    energy_ref, force_ref, coords_out, moving_out,
    feat_ref, side_ref, vec_ref, zc_ref, ze_ref, pos_ref, new_ref, sem, *work_refs,
    half, listed,
):
    first = near_ref[half * listed]
    take1 = near_ref[half * listed + 1] == 1
    take2 = near_ref[half * listed + 2] == 1
    dist_refs, mat_refs = work_refs[:RING], work_refs[RING:]

    def prepare(t, from_ref, at, own):
        def rows(ref, *js):
            return [ref[j, pl.ds(t, 1), :] for j in js]

        there = t + (first if own else half - first)
        dest = t if own else t + half
        charge0, depth0, h = [look_ref[j, pl.ds(there, 1), :] for j in range(3)]
        x, y, z, cpl0, cpl1 = rows(from_ref, *range(5))
        low0, low1 = rows(pair1_ref, at, at + 1)
        up0, up1 = rows(pair2_ref, at, at + 1)
        n = x * x + y * y + z * z
        h2 = h * h
        one = jnp.ones_like(n)
        zero = jnp.zeros_like(n)
        feats = jnp.concatenate([x, y, z, n, h, h2, one, zero], axis=0)
        p1, p2, p3 = split3(feats)
        feat_ref[dest] = jnp.concatenate([p1, p1, p2, p2, p1, p3], axis=0)
        c0 = charge0 * cpl0
        e0 = depth0 * cpl1
        pos = feats[0:3]
        zc = jnp.concatenate([c0, charge0 * low0, charge0 * up0, c0 * pos, zero, zero], axis=0)
        ze = jnp.concatenate([e0, depth0 * low1, depth0 * up1, e0 * pos, zero, zero], axis=0)
        c1, c2 = split2(zc)
        e1, e2 = split2(ze)
        vec_ref[dest] = jnp.concatenate([c1, c2, e1, e2], axis=0)
        if own:
            zc_ref[dest] = zc
            ze_ref[dest] = ze
            pos_ref[dest] = feats
            m = -2.0 * pos
            hh = 2.0 * h
            sides = jnp.concatenate(
                [
                    jnp.concatenate([m, one, zero, zero, n + DELTA_SOFT, zero], axis=0),
                    jnp.concatenate([m, one, hh, one, n + h2, zero], axis=0),
                    jnp.concatenate([zero, zero, zero, zero, hh, one, h2, zero], axis=0),
                ],
                axis=1,
            )
            q1, q2, q3 = split3(sides)
            side_ref[dest] = jnp.concatenate([q1, q2, q1, q2, q3, q1], axis=0)

    def prep_own(t, _):
        prepare(t, five_ref, 0, True)
        return 0

    def prep_other(t, _):
        prepare(t, other_ref, 2, False)
        return 0

    for j in range(6):
        mine = five_ref[j] if j < 3 else moving_ref[j - 3]
        new_ref[j // 3, j % 3] = jnp.where(
            take1, pair1_ref[4 + j], jnp.where(take2, pair2_ref[4 + j], mine)
        )
    copies = [
        pltpu.make_async_copy(new_ref.at[n], out, sem.at[n])
        for n, out in enumerate((coords_out, moving_out))
    ]
    for copy in copies:
        copy.start()
    lax.fori_loop(0, half, prep_own, 0, unroll=PREP)
    lax.fori_loop(0, half, prep_other, 0, unroll=PREP)

    def distances(i, k):
        c = near_ref[i * listed + k]
        dist_refs[k % RING][...] = lax.dot_general(
            feat_ref[c], side_ref[i], (((0,), (0,)), ((), ())),
            preferred_element_type=jnp.float32,
        )

    def functions(k):
        dist_ref, mat_ref = dist_refs[k % RING], mat_refs[k % RING]
        for r in range(0, TILE, CHUNK):
            rows = slice(r, r + CHUNK)
            low_rows = slice(TILE + r, TILE + r + CHUNK)
            s = dist_ref[rows, :TILE]
            t = dist_ref[rows, TILE : 2 * TILE]
            g = dist_ref[rows, 2 * TILE :]
            inv = lax.rsqrt(s)
            rt = 1.0 / t
            x = g * rt
            x3 = x * x * x
            f = x3 * (x3 - 0.5) * rt
            b = x3 * (x3 - 1.0)
            for n, mat in enumerate((inv, b, inv * inv * inv, f)):
                hi, lo = split2(mat)
                mat_ref[n, rows] = hi
                mat_ref[n, low_rows] = lo

    def gather(i, k, acc):
        vec = vec_ref[near_ref[i * listed + k]]
        cc = jnp.concatenate([vec[:16], vec[:16]], axis=1)
        ee = jnp.concatenate([vec[16:], vec[16:]], axis=1)
        mat_ref = mat_refs[k % RING]
        return [
            a + jnp.dot(lhs, mat_ref[n], preferred_element_type=jnp.float32)
            for n, (a, lhs) in enumerate(zip(acc, (cc, ee, cc, ee)))
        ]

    def finish(i, acc, total):
        sum_a, sum_b, sum_i, sum_f = [a[:8] + a[8:] for a in acc]
        own_times = jnp.int32(0)
        for k in range(listed):
            own_times = own_times + jnp.where(near_ref[i * listed + k] == i, 1, 0)
        zc = zc_ref[i]
        ze = ze_ref[i]
        own = own_times.astype(jnp.float32) * (DELTA_SOFT**-0.5)
        pos = pos_ref[i, 0:3]
        force = zc[0:1] * (pos * sum_i[0:1] - sum_i[3:6]) + 48.0 * ze[0:1] * (
            pos * sum_f[0:1] - sum_f[3:6]
        )
        for j in range(3):
            force_ref[j, pl.ds(i, 1), :] = force[j : j + 1]
        return total + zc * (sum_a - own * zc) + 4.0 * (ze * sum_b)

    def nothing():
        return [jnp.zeros((16, TILE), jnp.float32) for _ in range(4)]

    def row(i, acc, total):
        behind = jnp.maximum(i - 1, 0)
        following = jnp.minimum(i + 1, half - 1)
        for k in range(listed - LATE, listed):
            acc = gather(behind, k, acc)
        done = finish(behind, acc, total)
        total = jnp.where(i > 0, done, total)
        acc = nothing()
        for k in range(listed):
            if k + AHEAD < listed:
                distances(i, k + AHEAD)
            functions(k)
            if k + AHEAD >= listed:
                distances(following, k + AHEAD - listed)
            if k < listed - LATE:
                acc = gather(i, k, acc)
        return acc, total

    def next_rows(step, carry):
        for j in range(ROWS):
            carry = row(step * ROWS + j, *carry)
        return carry

    for k in range(AHEAD):
        distances(0, k)
    for k in range(listed - LATE, listed):
        mat_refs[k][...] = jnp.zeros_like(mat_refs[k])
    acc, total = lax.fori_loop(
        0, half // ROWS, next_rows, (nothing(), jnp.zeros((8, TILE), jnp.float32))
    )
    for k in range(listed - LATE, listed):
        acc = gather(half - 1, k, acc)
    total = finish(half - 1, acc, total)
    sums = jnp.sum(total, axis=1, keepdims=True) * (0.5 / (2 * half * TILE))
    is_odd = near_ref[half * listed + 3] == 1
    lower = jnp.where(is_odd, sums[1:2], sums[2:3])
    upper = jnp.where(is_odd, sums[2:3], sums[1:2])
    lane = lax.broadcasted_iota(jnp.int32, (1, TILE), 1)
    energy_ref[...] = jnp.where(lane == 0, sums[0:1], jnp.where(lane == 1, lower, upper))
    for copy in copies:
        copy.wait()


def lookup(charges, types, type_sigma, type_eps):
    levels = lax.broadcasted_iota(jnp.int32, (type_sigma.shape[0], types.shape[0]), 0)
    onehot = (levels == types[None, :]).astype(jnp.float32)
    table = jnp.stack([jnp.sqrt(type_eps), 0.5 * type_sigma])
    looked = jnp.dot(table, onehot, precision=lax.Precision.HIGHEST)
    return jnp.concatenate([charges[None], looked])


def call_kernel(args, half, listed):
    tiles = 2 * half
    vmem = pl.BlockSpec(memory_space=pltpu.VMEM)
    hbm = pl.BlockSpec(memory_space=pltpu.HBM)
    return pl.pallas_call(
        partial(tile_kernel, half=half, listed=listed),
        out_shape=(
            jax.ShapeDtypeStruct((1, TILE), jnp.float32),
            jax.ShapeDtypeStruct((3, half, TILE), jnp.float32),
            jax.ShapeDtypeStruct((3, half, TILE), jnp.float32),
            jax.ShapeDtypeStruct((3, half, TILE), jnp.float32),
        ),
        in_specs=[pl.BlockSpec(memory_space=pltpu.SMEM)] + [vmem] * 6,
        out_specs=(vmem, vmem, hbm, hbm),
        scratch_shapes=[
            pltpu.VMEM((tiles, 48, TILE), jnp.bfloat16),
            pltpu.VMEM((half, 48, 3 * TILE), jnp.bfloat16),
            pltpu.VMEM((tiles, 32, TILE), jnp.bfloat16),
            pltpu.VMEM((half, 8, TILE), jnp.float32),
            pltpu.VMEM((half, 8, TILE), jnp.float32),
            pltpu.VMEM((half, 8, TILE), jnp.float32),
            pltpu.VMEM((2, 3, half, TILE), jnp.float32),
            pltpu.SemaphoreType.DMA((2,)),
        ]
        + [pltpu.VMEM((TILE, 3 * TILE), jnp.float32)] * RING
        + [pltpu.VMEM((4, 2 * TILE, TILE), jnp.bfloat16)] * RING,
        compiler_params=pltpu.CompilerParams(vmem_limit_bytes=40 * 2**20),
        name="tiles",
    )(*args)


def per_device(
    coords, velocities, coupling, charges, types, type_sigma, type_eps, near_tiles, accept
):
    width = coords.shape[2]
    half = width // TILE
    listed = near_tiles.shape[1]
    pos = coords.reshape(3, half, TILE)
    moving = velocities.reshape(3, half, TILE)
    cpl = coupling.reshape(2, half, TILE)
    five = jnp.concatenate([pos, cpl])
    other = swapped(five, "atom", 0)
    look = lookup(charges, types, type_sigma, type_eps).reshape(3, 2 * half, TILE)
    first = lax.axis_index("atom") * half
    tiles = 2 * half
    local = jnp.mod(near_tiles.reshape(-1) - first + tiles, tiles)
    replica = lax.axis_index("lam")
    cycle = lax.axis_size("lam")
    odd = replica % 2
    flag1 = accept[replica - odd]
    flag2 = accept[jnp.mod(replica - 1 + odd + cycle, cycle)]
    near = jnp.concatenate([local, jnp.stack([first, flag1, flag2, odd])]).astype(jnp.int32)

    other, look, near = lax.optimization_barrier((other, look, near))
    ten = jnp.concatenate([cpl, other[3:], pos, moving])
    pair1 = swapped(ten, "lam", 0)
    pair2 = swapped(ten, "lam", 1)

    energy, force, new_coords, new_velocities = call_kernel(
        (near, five, moving, other, pair1, pair2, look), half, listed
    )
    part = energy[:, :3]
    shape = coords.shape
    return (
        part + swapped(part, "atom", 0),
        force.reshape(shape),
        new_coords.reshape(shape),
        new_velocities.reshape(shape),
    )


def solution(mesh):
    in_specs = (
        P("lam", None, "atom"),
        P("lam", None, "atom"),
        P("lam", None, "atom"),
        P(),
        P(),
        P(),
        P(),
        P("atom", None),
        P(),
    )
    out_specs = (
        P("lam", None),
        P("lam", None, "atom"),
        P("lam", None, "atom"),
        P("lam", None, "atom"),
    )
    return jax.shard_map(
        per_device, mesh=mesh, in_specs=in_specs, out_specs=out_specs, check_vma=False
    )
```

```python
from functools import partial

import jax
import jax.numpy as jnp
from jax import lax
from jax.experimental import pallas as pl
from jax.experimental.pallas import tpu as pltpu
from jax.sharding import PartitionSpec as P

TILE = 128
DELTA_SOFT = 0.05
CHUNK = 32
RING = 5
AHEAD = 3
LATE = 2
ROWS = 16
PREP = 8


def swapped(x, axis, first):
    peers = lax.axis_size(axis)
    pairs = []
    for i in range(first, peers + first, 2):
        low, high = i % peers, (i + 1) % peers
        pairs += [(low, high), (high, low)]
    return lax.ppermute(x, axis, pairs)


def split3(z):
    one = z.astype(jnp.bfloat16)
    rest = z - one.astype(jnp.float32)
    two = rest.astype(jnp.bfloat16)
    rest = rest - two.astype(jnp.float32)
    return one, two, rest.astype(jnp.bfloat16)


def split2(z):
    one = z.astype(jnp.bfloat16)
    two = (z - one.astype(jnp.float32)).astype(jnp.bfloat16)
    return one, two


def place_kernel(
    info_ref, own_ref, other_ref, look_ref, feat_ref, side_ref, pos_ref, *, half
):
    first = info_ref[0]

    def prepare(t, from_ref, own):
        there = t + (first if own else half - first)
        dest = t if own else t + half
        h = look_ref[2, pl.ds(there, 1), :]
        x, y, z = [from_ref[j, pl.ds(t, 1), :] for j in range(2, 5)]
        n = x * x + y * y + z * z
        h2 = h * h
        one = jnp.ones_like(n)
        zero = jnp.zeros_like(n)
        feats = jnp.concatenate([x, y, z, n, h, h2, one, zero], axis=0)
        p1, p2, p3 = split3(feats)
        feat_ref[dest] = jnp.concatenate([p1, p1, p2, p2, p1, p3], axis=0)
        if own:
            pos_ref[dest] = feats
            m = -2.0 * feats[0:3]
            hh = 2.0 * h
            sides = jnp.concatenate(
                [
                    jnp.concatenate([m, one, zero, zero, n + DELTA_SOFT, zero], axis=0),
                    jnp.concatenate([m, one, hh, one, n + h2, zero], axis=0),
                    jnp.concatenate([zero, zero, zero, zero, hh, one, h2, zero], axis=0),
                ],
                axis=1,
            )
            q1, q2, q3 = split3(sides)
            side_ref[dest] = jnp.concatenate([q1, q2, q1, q2, q3, q1], axis=0)

    def prep_own(t, _):
        prepare(t, own_ref, True)
        return 0

    def prep_other(t, _):
        prepare(t, other_ref, False)
        return 0

    lax.fori_loop(0, half, prep_own, 0, unroll=PREP)
    lax.fori_loop(0, half, prep_other, 0, unroll=PREP)


def tile_kernel(
    near_ref, info_ref,
    own_ref, other_ref, pair1_ref, pair2_ref, far_ref, look_ref, feat_ref, side_ref, pos_ref,
    energy_ref, force_ref, coords_out, moving_out,
    vec_ref, zc_ref, ze_ref, new_ref, sem, *work_refs,
    half, listed,
):
    first = info_ref[0]
    take1 = info_ref[1] == 1
    take2 = info_ref[2] == 1
    dist_refs, mat_refs = work_refs[:RING], work_refs[RING:]

    def listed_tile(i, k):
        c = near_ref[i, k] - first
        return jnp.where(c < 0, c + 2 * half, c)

    def prepare(t, own):
        from_ref = own_ref if own else other_ref
        there = t + (first if own else half - first)
        dest = t if own else t + half

        def row(ref, j):
            return ref[j, pl.ds(t, 1), :]

        charge0, depth0 = [look_ref[j, pl.ds(there, 1), :] for j in range(2)]
        cpl0, cpl1, x, y, z = [row(from_ref, j) for j in range(5)]
        if own:
            one0, one1, two0, two1 = [row(r, j) for r in (pair1_ref, pair2_ref) for j in range(2)]
        else:
            one0, one1, two0, two1 = [row(far_ref, j) for j in range(4)]
        zero = jnp.zeros_like(x)
        c0 = charge0 * cpl0
        e0 = depth0 * cpl1
        zc = jnp.concatenate(
            [c0, charge0 * one0, charge0 * two0, c0 * x, c0 * y, c0 * z, zero, zero], axis=0
        )
        ze = jnp.concatenate(
            [e0, depth0 * one1, depth0 * two1, e0 * x, e0 * y, e0 * z, zero, zero], axis=0
        )
        c1, c2 = split2(zc)
        e1, e2 = split2(ze)
        vec_ref[dest] = jnp.concatenate([c1, c2, e1, e2], axis=0)
        if own:
            zc_ref[dest] = zc
            ze_ref[dest] = ze

    def prep_own(t, _):
        prepare(t, True)
        return 0

    def prep_other(t, _):
        prepare(t, False)
        return 0

    for j in range(6):
        new_ref[j // 3, j % 3] = jnp.where(
            take1, pair1_ref[2 + j], jnp.where(take2, pair2_ref[2 + j], own_ref[2 + j])
        )
    copies = [
        pltpu.make_async_copy(new_ref.at[n], out, sem.at[n])
        for n, out in enumerate((coords_out, moving_out))
    ]
    for copy in copies:
        copy.start()
    lax.fori_loop(0, half, prep_own, 0, unroll=PREP)
    lax.fori_loop(0, half, prep_other, 0, unroll=PREP)

    def distances(i, k):
        c = listed_tile(i, k)
        dist_refs[k % RING][...] = lax.dot_general(
            feat_ref[c], side_ref[i], (((0,), (0,)), ((), ())),
            preferred_element_type=jnp.float32,
        )

    def functions(k):
        dist_ref, mat_ref = dist_refs[k % RING], mat_refs[k % RING]
        for r in range(0, TILE, CHUNK):
            rows = slice(r, r + CHUNK)
            low_rows = slice(TILE + r, TILE + r + CHUNK)
            s = dist_ref[rows, :TILE]
            t = dist_ref[rows, TILE : 2 * TILE]
            g = dist_ref[rows, 2 * TILE :]
            inv = lax.rsqrt(s)
            rt = 1.0 / t
            x = g * rt
            x3 = x * x * x
            f = x3 * (x3 - 0.5) * rt
            b = x3 * (x3 - 1.0)
            for n, mat in enumerate((inv, b, inv * inv * inv, f)):
                hi, lo = split2(mat)
                mat_ref[n, rows] = hi
                mat_ref[n, low_rows] = lo

    def gather(i, k, acc):
        vec = vec_ref[listed_tile(i, k)]
        cc = jnp.concatenate([vec[:16], vec[:16]], axis=1)
        ee = jnp.concatenate([vec[16:], vec[16:]], axis=1)
        mat_ref = mat_refs[k % RING]
        return [
            a + jnp.dot(lhs, mat_ref[n], preferred_element_type=jnp.float32)
            for n, (a, lhs) in enumerate(zip(acc, (cc, ee, cc, ee)))
        ]

    def finish(i, acc, total):
        sum_a, sum_b, sum_i, sum_f = [a[:8] + a[8:] for a in acc]
        own_times = jnp.int32(0)
        for k in range(listed):
            own_times = own_times + jnp.where(listed_tile(i, k) == i, 1, 0)
        zc = zc_ref[i]
        ze = ze_ref[i]
        own = own_times.astype(jnp.float32) * (DELTA_SOFT**-0.5)
        pos = pos_ref[i, 0:3]
        force = zc[0:1] * (pos * sum_i[0:1] - sum_i[3:6]) + 48.0 * ze[0:1] * (
            pos * sum_f[0:1] - sum_f[3:6]
        )
        for j in range(3):
            force_ref[j, pl.ds(i, 1), :] = force[j : j + 1]
        return total + zc * (sum_a - own * zc) + 4.0 * (ze * sum_b)

    def nothing():
        return [jnp.zeros((16, TILE), jnp.float32) for _ in range(4)]

    def row(i, acc, total):
        behind = jnp.maximum(i - 1, 0)
        following = jnp.minimum(i + 1, half - 1)
        for k in range(listed - LATE, listed):
            acc = gather(behind, k, acc)
        done = finish(behind, acc, total)
        total = jnp.where(i > 0, done, total)
        acc = nothing()
        for k in range(listed):
            if k + AHEAD < listed:
                distances(i, k + AHEAD)
            functions(k)
            if k + AHEAD >= listed:
                distances(following, k + AHEAD - listed)
            if k < listed - LATE:
                acc = gather(i, k, acc)
        return acc, total

    def next_rows(step, carry):
        for j in range(ROWS):
            carry = row(step * ROWS + j, *carry)
        return carry

    for k in range(AHEAD):
        distances(0, k)
    for k in range(listed - LATE, listed):
        mat_refs[k][...] = jnp.zeros_like(mat_refs[k])
    acc, total = lax.fori_loop(
        0, half // ROWS, next_rows, (nothing(), jnp.zeros((8, TILE), jnp.float32))
    )
    for k in range(listed - LATE, listed):
        acc = gather(half - 1, k, acc)
    total = finish(half - 1, acc, total)
    sums = jnp.sum(total, axis=1, keepdims=True) * (0.5 / (2 * half * TILE))
    is_odd = info_ref[3] == 1
    lower = jnp.where(is_odd, sums[1:2], sums[2:3])
    upper = jnp.where(is_odd, sums[2:3], sums[1:2])
    lane = lax.broadcasted_iota(jnp.int32, (1, TILE), 1)
    energy_ref[...] = jnp.where(lane == 0, sums[0:1], jnp.where(lane == 1, lower, upper))
    for copy in copies:
        copy.wait()


def lookup(charges, types, type_sigma, type_eps):
    levels = lax.broadcasted_iota(jnp.int32, (type_sigma.shape[0], types.shape[0]), 0)
    onehot = (levels == types[None, :]).astype(jnp.float32)
    table = jnp.stack([jnp.sqrt(type_eps), 0.5 * type_sigma])
    looked = jnp.dot(table, onehot, precision=lax.Precision.HIGHEST)
    return jnp.concatenate([charges[None], looked])


def call_kernels(near, info, own, other, pair1, pair2, far, look):
    half, listed = near.shape
    tiles = 2 * half
    vmem = pl.BlockSpec(memory_space=pltpu.VMEM)
    smem = pl.BlockSpec(memory_space=pltpu.SMEM)
    hbm = pl.BlockSpec(memory_space=pltpu.HBM)
    limit = pltpu.CompilerParams(vmem_limit_bytes=40 * 2**20)
    feat, side, pos = pl.pallas_call(
        partial(place_kernel, half=half),
        out_shape=(
            jax.ShapeDtypeStruct((tiles, 48, TILE), jnp.bfloat16),
            jax.ShapeDtypeStruct((half, 48, 3 * TILE), jnp.bfloat16),
            jax.ShapeDtypeStruct((half, 8, TILE), jnp.float32),
        ),
        in_specs=[smem, vmem, vmem, vmem],
        out_specs=(vmem, vmem, vmem),
        compiler_params=limit,
        name="places",
    )(info, own, other, look)
    return pl.pallas_call(
        partial(tile_kernel, half=half, listed=listed),
        out_shape=(
            jax.ShapeDtypeStruct((1, TILE), jnp.float32),
            jax.ShapeDtypeStruct((3, half, TILE), jnp.float32),
            jax.ShapeDtypeStruct((3, half, TILE), jnp.float32),
            jax.ShapeDtypeStruct((3, half, TILE), jnp.float32),
        ),
        in_specs=[smem, smem] + [vmem] * 9,
        out_specs=(vmem, vmem, hbm, hbm),
        scratch_shapes=[
            pltpu.VMEM((tiles, 32, TILE), jnp.bfloat16),
            pltpu.VMEM((half, 8, TILE), jnp.float32),
            pltpu.VMEM((half, 8, TILE), jnp.float32),
            pltpu.VMEM((2, 3, half, TILE), jnp.float32),
            pltpu.SemaphoreType.DMA((2,)),
        ]
        + [pltpu.VMEM((TILE, 3 * TILE), jnp.float32)] * RING
        + [pltpu.VMEM((4, 2 * TILE, TILE), jnp.bfloat16)] * RING,
        compiler_params=limit,
        name="tiles",
    )(near, info, own, other, pair1, pair2, far, look, feat, side, pos)


def per_device(
    coords, velocities, coupling, charges, types, type_sigma, type_eps, near_tiles, accept
):
    half = coords.shape[2] // TILE
    own = jnp.concatenate(
        [
            coupling.reshape(2, half, TILE),
            coords.reshape(3, half, TILE),
            velocities.reshape(3, half, TILE),
        ]
    )
    pair2 = swapped(own, "lam", 1)
    pair1 = swapped(own, "lam", 0)
    other = swapped(own[:5], "atom", 0)

    look = lookup(charges, types, type_sigma, type_eps).reshape(3, 2 * half, TILE)
    replica = lax.axis_index("lam")
    cycle = lax.axis_size("lam")
    odd = replica % 2
    flag1 = accept[replica - odd]
    flag2 = accept[jnp.mod(replica - 1 + odd + cycle, cycle)]
    info = jnp.stack([lax.axis_index("atom") * half, flag1, flag2, odd]).astype(jnp.int32)

    pair1, pair2, other, look, info = lax.optimization_barrier((pair1, pair2, other, look, info))
    far = swapped(jnp.concatenate([pair1[:2], pair2[:2]]), "atom", 0)
    energy, force, new_coords, new_velocities = call_kernels(
        near_tiles, info, own, other, pair1, pair2, far, look
    )
    part = energy[:, :3]
    shape = coords.shape
    return (
        part + swapped(part, "atom", 0),
        force.reshape(shape),
        new_coords.reshape(shape),
        new_velocities.reshape(shape),
    )


def solution(mesh):
    in_specs = (
        P("lam", None, "atom"),
        P("lam", None, "atom"),
        P("lam", None, "atom"),
        P(),
        P(),
        P(),
        P(),
        P("atom", None),
        P(),
    )
    out_specs = (
        P("lam", None),
        P("lam", None, "atom"),
        P("lam", None, "atom"),
        P("lam", None, "atom"),
    )
    return jax.shard_map(
        per_device, mesh=mesh, in_specs=in_specs, out_specs=out_specs, check_vma=False
    )
```
